32 devices in a mesh: dp: 16 (over z, y, core), tensor: 2 (over x).
Axes of the slice: x: 2, y: 2, z: 4, core: 2. Of those that a mesh axis runs over, the one named last changes fastest.
Arguments:
- layer_in: bfloat16 [8192, 768], P(('dp', 'tensor')), may hold values from -6 to 6
- cotangent: bfloat16 [8192, 768], P(('dp', 'tensor')), may hold values from -6 to 6
- lengths: int32 [16], replicated, may hold values from 32 to 512, as said below
- slot_sequence: int32 [16], P('dp'), may hold values from 0 to 15, each once
- input_proj: bfloat16 [768, 3, 768], P('dp', None, 'tensor'), may hold values from -0.21875 to 0.21875
- query_bias: float32 [768], replicated, may hold values from -3 to 3
- value_bias: float32 [768], replicated, may hold values from -3 to 3
- output_proj: bfloat16 [768, 768], P('tensor', 'dp'), may hold values from -3.5 to 3.5
- output_bias: float32 [768], replicated, may hold values from -3 to 3
- first_gain: float32 [768], replicated, may hold values from 0.5 to 1.5
- first_shift: float32 [768], replicated, may hold values from -3 to 3
- up_proj: bfloat16 [768, 3072], P('dp', 'tensor'), may hold values from -0.21875 to 0.21875
- up_bias: float32 [3072], replicated, may hold values from -3 to 3
- down_proj: bfloat16 [3072, 768], P('tensor', 'dp'), may hold values from -0.109375 to 0.109375
- down_bias: float32 [768], replicated, may hold values from -3 to 3
- second_gain: float32 [768], replicated, may hold values from 0.5 to 1.5
- second_shift: float32 [768], replicated, may hold values from -3 to 3
Outputs:
- layer_out: bfloat16 [8192, 768], P(('dp', 'tensor'))
- input_grad: float32 [8192, 768], P(('dp', 'tensor'))
- input_proj_grad: float32 [768, 3, 768], P('dp', None, 'tensor')
- query_bias_grad: float32 [768], replicated
- value_bias_grad: float32 [768], replicated
- output_proj_grad: float32 [768, 768], P('tensor', 'dp')
- output_bias_grad: float32 [768], replicated
- first_gain_grad: float32 [768], replicated
- first_shift_grad: float32 [768], replicated
- up_proj_grad: float32 [768, 3072], P('dp', 'tensor')
- up_bias_grad: float32 [3072], replicated
- down_proj_grad: float32 [3072, 768], P('tensor', 'dp')
- down_bias_grad: float32 [768], replicated
- second_gain_grad: float32 [768], replicated
- second_shift_grad: float32 [768], replicated
The draws below stay inside these ranges and needn't reach their ends.
Inputs may be any that keep to these rules, and one draw needn't show every extreme that they name: `lengths`: the longest sequence has exactly 512 tokens. `slot_sequence`: each sequence fills exactly one slot.
All inputs are finite; a program needn't handle non-finite values.
Results may differ from the reference program's by a relative error of at most 0.015.
Values may be sent and summed in bfloat16 or wider, within the bound.
No kernel may reach another device: no remote copies, remote signals or barrier semaphores. Data moves between devices by JAX's collectives and lax.ppermute only.
A program may use at most 128 MiB of HBM per device.

```python
import math
import jax
import jax.numpy as jnp
from jax import lax

D = 768
HEADS = 12
HEAD_DIM = 64
FF = 3072
SLOT = 512
SEQS = 16
TOKENS = 8192


def draw_lengths(key, part):
    base_key, pick_key = jax.random.split(key)
    lowest = max(SLOT // 16, 1)
    values_drawn = jax.random.randint(base_key, (SEQS,), lowest, SLOT + 1)
    longest = jax.random.randint(pick_key, (), 0, SEQS)
    return jnp.where(jnp.arange(SEQS) == longest, SLOT, values_drawn).astype(jnp.int32)


def level_of(own_key, shape, pieces, smallest, top_value):
    loudness, own = 1.0, jax.random.fold_in(own_key, 6)
    for dim, shards_of in pieces:
        heights = jnp.exp(jax.random.uniform(jax.random.fold_in(own, dim), (shards_of,), jnp.float32, smallest / len(pieces), top_value / len(pieces)))
        loudness = loudness * jnp.repeat(heights, shape[dim] // shards_of).reshape([-1 if axis == dim else 1 for axis in range(len(shape))])
    return loudness


def gaussian(own_key, extent, scale, limit, pieces=(), held_as=jnp.bfloat16):
    factor_of = level_of(own_key, extent, pieces, -0.22, 0.18) if pieces else 1.0
    values = jax.random.normal(own_key, extent, jnp.float32) * scale * factor_of
    return jnp.minimum(jnp.maximum(values, -limit), limit).astype(held_as)


def setup_inputs(seed: int = 0) -> dict:
    splits = jax.random.split(jax.random.key(seed), 18)
    layer_in = gaussian(splits[0], (TOKENS, D), 1.0, 6.0, ((0, 32),))
    cotangent = gaussian(splits[1], (TOKENS, D), 1.0, 6.0, ((0, 32),))
    lengths = draw_lengths(jax.random.fold_in(splits[17], 71), 0)
    slot_sequence = jax.random.permutation(splits[3], SEQS).astype(jnp.int32)
    input_proj = gaussian(splits[4], (D, 3, D), D ** -0.5, 0.21875, ((0, 16), (2, 2)))
    query_bias = gaussian(splits[5], (D,), 0.5, 3.0, (), jnp.float32)
    value_bias = gaussian(splits[6], (D,), 0.5, 3.0, (), jnp.float32)
    output_proj = gaussian(splits[7], (D, D), (max(2 * D // SLOT, 1)) ** -0.5, 3.5, ((0, 2), (1, 16)))
    output_bias = gaussian(splits[8], (D,), 0.5, 3.0, (), jnp.float32)
    first_gain = jnp.clip(1.0 + 0.1 * jax.random.normal(splits[9], (D,), jnp.float32), 0.5, 1.5)
    first_shift = gaussian(splits[10], (D,), 0.5, 3.0, (), jnp.float32)
    up_proj = gaussian(splits[11], (D, FF), D ** -0.5, 0.21875, ((0, 16), (1, 2)))
    up_bias = gaussian(splits[12], (FF,), 0.5, 3.0, (), jnp.float32)
    down_proj = gaussian(splits[13], (FF, D), FF ** -0.5, 0.109375, ((0, 2), (1, 16)))
    down_bias = gaussian(splits[14], (D,), 0.5, 3.0, (), jnp.float32)
    second_gain = jnp.clip(1.0 + 0.1 * jax.random.normal(splits[15], (D,), jnp.float32), 0.5, 1.5)
    second_shift = gaussian(splits[16], (D,), 0.5, 3.0, (), jnp.float32)
    return {"layer_in": layer_in, "cotangent": cotangent, "lengths": lengths, "slot_sequence": slot_sequence, "input_proj": input_proj, "query_bias": query_bias, "value_bias": value_bias, "output_proj": output_proj, "output_bias": output_bias, "first_gain": first_gain, "first_shift": first_shift, "up_proj": up_proj, "up_bias": up_bias, "down_proj": down_proj, "down_bias": down_bias, "second_gain": second_gain, "second_shift": second_shift}


EPSILON = 1e-05
ROOT_HALF = 0.7071067811865476
INV_ROOT_TAU = 0.3989422804014327

def norm_forward(values, gain, shift):
    centered = values - lax.optimization_barrier(jnp.mean(values, axis=-1, keepdims=True))
    inv_std = lax.rsqrt(lax.optimization_barrier(jnp.mean(centered * centered, axis=-1, keepdims=True)) + EPSILON)
    normed = centered * inv_std
    return (normed * gain + shift, normed, inv_std)

def norm_backward(upstream, normed, inv_std, gain):
    scaled = upstream * gain
    return inv_std * (scaled - lax.optimization_barrier(jnp.mean(scaled, axis=-1, keepdims=True)) - normed * lax.optimization_barrier(jnp.mean(scaled * normed, axis=-1, keepdims=True)))

def gelu_value(inputs):
    return inputs * 0.5 * (1.0 + lax.erf(inputs * ROOT_HALF))

def gelu_slope(inputs):
    return 0.5 * (1.0 + lax.erf(inputs * ROOT_HALF)) + inputs * jnp.exp(-0.5 * inputs * inputs) * INV_ROOT_TAU

def rounded_copy(values):
    return lax.optimization_barrier(values.astype(jnp.bfloat16)).astype(jnp.float32)

def attend_forward(queries, key_rows, values, length):
    factor = 1.0 / math.sqrt(HEAD_DIM)
    scores = jnp.einsum('qhd,khd->hqk', queries.astype(jnp.float32), key_rows.astype(jnp.float32)) * factor
    visible = jnp.arange(SLOT) < length
    log_total = jnp.log(lax.optimization_barrier(jnp.sum(jnp.where(visible, jnp.exp(scores), 0.0), axis=-1)))
    probability = jnp.where(visible, jnp.exp(scores - log_total[:, :, None]), 0.0)
    context = jnp.einsum('hqk,khd->qhd', rounded_copy(probability), values.astype(jnp.float32))
    return (context.astype(jnp.bfloat16), log_total)

def attend_backward(queries, key_rows, values, length, log_total, grad_context):
    factor = 1.0 / math.sqrt(HEAD_DIM)
    query_wide = queries.astype(jnp.float32)
    key_wide = key_rows.astype(jnp.float32)
    grad_wide = grad_context.astype(jnp.float32)
    scores = jnp.einsum('qhd,khd->hqk', query_wide, key_wide) * factor
    visible = jnp.arange(SLOT) < length
    probability = jnp.where(visible, jnp.exp(scores - log_total[:, :, None]), 0.0)
    grad_prob = jnp.einsum('qhd,khd->hqk', grad_wide, values.astype(jnp.float32))
    inner_sum = lax.optimization_barrier(jnp.sum(probability * grad_prob, axis=-1, keepdims=True))
    grad_score = rounded_copy(probability * (grad_prob - inner_sum))
    grad_query = jnp.einsum('hqk,khd->qhd', grad_score, key_wide) * factor
    grad_key = jnp.einsum('hqk,qhd->khd', grad_score, query_wide) * factor
    grad_value = jnp.einsum('hqk,qhd->khd', rounded_copy(probability), grad_wide)
    return (grad_query, grad_key, grad_value)

def reference(layer_in, cotangent, lengths, slot_sequence, input_proj, query_bias, value_bias, output_proj, output_bias, first_gain, first_shift, up_proj, up_bias, down_proj, down_bias, second_gain, second_shift):
    flat_in = input_proj.reshape(D, 3 * D)
    proj_bias = jnp.stack([query_bias, jnp.zeros_like(query_bias), value_bias])
    slot_length = lengths[slot_sequence]
    grad_scale = 1.0 / math.sqrt(TOKENS)

    def one_sequence(totals, inputs):
        seq_rows, seq_cotan, length = inputs
        projected = jnp.dot(seq_rows, flat_in, preferred_element_type=jnp.float32).reshape(SLOT, 3, D) + proj_bias
        head_split = projected.astype(jnp.bfloat16).reshape(SLOT, 3, HEADS, HEAD_DIM)
        queries = head_split[:, 0]
        key_rows = head_split[:, 1]
        values = head_split[:, 2]
        context, log_total = attend_forward(queries, key_rows, values, length)
        context_flat = context.reshape(SLOT, D)
        residual = seq_rows.astype(jnp.float32) + jnp.dot(context_flat, output_proj, preferred_element_type=jnp.float32) + output_bias
        middle, normed_one, inv_one = norm_forward(residual, first_gain, first_shift)
        middle_b = middle.astype(jnp.bfloat16)
        pre_active = jnp.dot(middle_b, up_proj, preferred_element_type=jnp.float32) + up_bias
        active = gelu_value(pre_active).astype(jnp.bfloat16)
        summed = middle + jnp.dot(active, down_proj, preferred_element_type=jnp.float32) + down_bias
        result, normed_two, inv_two = norm_forward(summed, second_gain, second_shift)
        upstream = seq_cotan.astype(jnp.float32)
        grad_summed = norm_backward(upstream, normed_two, inv_two, second_gain)
        summed_b = grad_summed.astype(jnp.bfloat16)
        grad_active = jnp.dot(summed_b, down_proj.T, preferred_element_type=jnp.float32)
        grad_pre = grad_active * gelu_slope(pre_active)
        pre_b = grad_pre.astype(jnp.bfloat16)
        grad_middle = grad_summed + jnp.dot(pre_b, up_proj.T, preferred_element_type=jnp.float32)
        grad_residual = norm_backward(grad_middle, normed_one, inv_one, first_gain)
        residual_b = grad_residual.astype(jnp.bfloat16)
        grad_context = jnp.dot(residual_b, output_proj.T, preferred_element_type=jnp.float32).astype(jnp.bfloat16)
        grad_context = grad_context.reshape(SLOT, HEADS, HEAD_DIM)
        grad_query, grad_key, grad_value = attend_backward(queries, key_rows, values, length, log_total, grad_context)
        grad_proj = jnp.stack([grad_query, grad_key, grad_value], axis=1).reshape(SLOT, 3 * D)
        proj_b = grad_proj.astype(jnp.bfloat16)
        grad_rows = grad_residual + jnp.dot(proj_b, flat_in.T, preferred_element_type=jnp.float32)
        gradient_terms = (jnp.dot(seq_rows.T, proj_b, preferred_element_type=jnp.float32).reshape(D, 3, D), lax.optimization_barrier(jnp.sum(grad_query, axis=0)).reshape(D), lax.optimization_barrier(jnp.sum(grad_value, axis=0)).reshape(D), jnp.dot(context_flat.T, residual_b, preferred_element_type=jnp.float32), lax.optimization_barrier(jnp.sum(grad_residual, axis=0)), lax.optimization_barrier(jnp.sum(grad_middle * normed_one, axis=0)), lax.optimization_barrier(jnp.sum(grad_middle, axis=0)), jnp.dot(middle_b.T, pre_b, preferred_element_type=jnp.float32), lax.optimization_barrier(jnp.sum(grad_pre, axis=0)), jnp.dot(active.T, summed_b, preferred_element_type=jnp.float32), lax.optimization_barrier(jnp.sum(grad_summed, axis=0)), lax.optimization_barrier(jnp.sum(upstream * normed_two, axis=0)), lax.optimization_barrier(jnp.sum(upstream, axis=0)))
        updated = jax.tree.map(jnp.add, totals, gradient_terms)
        return (updated, (result.astype(jnp.bfloat16), grad_rows))
    starting = (jnp.zeros((D, 3, D), jnp.float32), jnp.zeros((D,), jnp.float32), jnp.zeros((D,), jnp.float32), jnp.zeros((D, D), jnp.float32), jnp.zeros((D,), jnp.float32), jnp.zeros((D,), jnp.float32), jnp.zeros((D,), jnp.float32), jnp.zeros((D, FF), jnp.float32), jnp.zeros((FF,), jnp.float32), jnp.zeros((FF, D), jnp.float32), jnp.zeros((D,), jnp.float32), jnp.zeros((D,), jnp.float32), jnp.zeros((D,), jnp.float32))
    totals, (outputs, grads) = lax.scan(one_sequence, starting, (layer_in.reshape(SEQS, SLOT, D), cotangent.reshape(SEQS, SLOT, D), slot_length))
    return (outputs.reshape(TOKENS, D), grads.reshape(TOKENS, D), totals[0] * grad_scale, totals[1] * grad_scale, totals[2] * grad_scale, totals[3] * grad_scale, totals[4] * grad_scale, totals[5] * grad_scale, totals[6] * grad_scale, totals[7] * grad_scale, totals[8] * grad_scale, totals[9] * grad_scale, totals[10] * grad_scale, totals[11] * grad_scale, totals[12] * grad_scale)
```

```python
import math

import jax
import jax.numpy as jnp
import numpy as np
from jax import lax
from jax.sharding import PartitionSpec as P

HEAD_DIM = 64
CHUNKS = 2
EPSILON = 1e-05
ROOT_HALF = 0.7071067811865476
INV_ROOT_TAU = 0.3989422804014327


BF16 = jnp.bfloat16
F32 = jnp.float32


def phases_of(count):
    phases, stride = [], 1
    for radix in [2] + ([2] if math.log2(count // 2) % 2 else []):
        if count // stride >= radix:
            phases.append((stride, radix))
            stride *= radix
    while stride < count:
        radix = min(4, count // stride)
        phases.append((stride, radix))
        stride *= radix
    return phases


def block_order(phases):
    order = [0]
    for stride, radix in reversed(phases):
        order = [old ^ (step * stride) for step in range(radix) for old in order]
    return order


def swap(value, distance):
    count = lax.axis_size("dp")
    return lax.ppermute(value, "dp", [(i, i ^ distance) for i in range(count)])


def swap_pair(value):
    return lax.ppermute(value, "tensor", [(0, 1), (1, 0)])


def gather_rows(shard, phases):
    held = shard
    for stride, radix in reversed(phases):
        held = jnp.concatenate(
            [held] + [swap(held, step * stride) for step in range(1, radix)], axis=0
        )
    return held


def tree_sum(parts):
    while len(parts) > 1:
        parts = [parts[i] + parts[i + 1] for i in range(0, len(parts), 2)]
    return parts[0]


def scatter_rows(total, phases):
    for stride, radix in phases:
        size = total.shape[0] // radix
        parts = [total[:size]]
        for step in range(1, radix):
            piece = total[step * size : (step + 1) * size].astype(BF16)
            parts.append(swap(piece, step * stride).astype(F32))
        total = tree_sum(parts)
    return total


def all_sum(vector, phases):
    for stride, radix in phases:
        vector = tree_sum(
            [vector] + [swap(vector, step * stride) for step in range(1, radix)]
        )
    return vector + swap_pair(vector)


def norm_forward(values):
    centered = values - jnp.mean(values, axis=-1, keepdims=True)
    inv_std = lax.rsqrt(jnp.mean(centered * centered, axis=-1, keepdims=True) + EPSILON)
    return centered * inv_std, inv_std


def norm_backward(upstream, normed, inv_std, gain):
    scaled = upstream * gain
    return inv_std * (
        scaled
        - jnp.mean(scaled, axis=-1, keepdims=True)
        - normed * jnp.mean(scaled * normed, axis=-1, keepdims=True)
    )


def dot(left, right, dims=((1,), (0,))):
    return lax.dot_general(left, right, (dims, ((), ())), preferred_element_type=F32)


def placed(vector, total_size, start_at):
    return lax.dynamic_update_slice_in_dim(jnp.zeros((total_size,), F32), vector, start_at, 0)


def local(
    layer_in,
    cotangent,
    lengths,
    slot_sequence,
    input_proj,
    query_bias,
    value_bias,
    output_proj,
    output_bias,
    first_gain,
    first_shift,
    up_proj,
    up_bias,
    down_proj,
    down_bias,
    second_gain,
    second_shift,
):
    me = lax.axis_index("dp")
    member = lax.axis_index("tensor")
    count = lax.axis_size("dp")
    phases = phases_of(count)
    local_rows, width = layer_in.shape
    seq_len = local_rows * 2
    half_width = input_proj.shape[2]
    heads = half_width // HEAD_DIM
    hidden_half = up_proj.shape[1]
    block = input_proj.shape[0]
    grad_scale = 1.0 / math.sqrt(seq_len * count)
    offset = member * half_width
    hidden_offset = member * hidden_half
    length = jnp.sum(jnp.where(jnp.arange(lengths.shape[0]) == slot_sequence[0], lengths, 0))

    order = np.repeat(np.asarray(block_order(phases), np.int32), block)
    source = (me ^ order) * block + np.arange(width, dtype=np.int32) % block
    pick = (jnp.arange(width)[:, None] == source[None, :]).astype(BF16)

    def to_own(values):
        return dot(values, pick).astype(BF16)

    def exact(values, dims):
        return lax.dot_general(
            values,
            pick.astype(F32),
            (dims, ((), ())),
            precision=lax.Precision.HIGHEST,
            preferred_element_type=F32,
        )

    in_rows = gather_rows(input_proj.reshape(block, 3 * half_width), phases)
    out_rows = gather_rows(output_proj.T, phases)
    up_rows = gather_rows(up_proj, phases)
    down_rows = gather_rows(down_proj.T, phases)

    vectors = exact(
        jnp.stack([output_bias, first_gain, first_shift, down_bias, second_gain, second_shift]),
        ((1,), (0,)),
    )
    out_bias, gain_one, shift_one, low_bias, gain_two, shift_two = vectors

    def both(mine):
        other = swap_pair(mine)
        first = member == 0
        return jnp.concatenate([jnp.where(first, mine, other), jnp.where(first, other, mine)])

    rows_in = both(to_own(layer_in))
    rows_cotan = both(to_own(cotangent))

    proj_bias = jnp.concatenate(
        [
            lax.dynamic_slice_in_dim(query_bias, offset, half_width),
            jnp.zeros((half_width,), F32),
            lax.dynamic_slice_in_dim(value_bias, offset, half_width),
        ]
    )
    local_up_bias = lax.dynamic_slice_in_dim(up_bias, hidden_offset, hidden_half)

    projected = (dot(rows_in, in_rows) + proj_bias).astype(BF16)
    split = projected.reshape(seq_len, 3, heads, HEAD_DIM)
    queries, keys, values = split[:, 0], split[:, 1], split[:, 2]
    factor = 1.0 / math.sqrt(HEAD_DIM)
    visible = jnp.arange(seq_len) < length
    scores = jnp.einsum("qhd,khd->hqk", queries, keys, preferred_element_type=F32) * factor
    log_total = jnp.log(jnp.sum(jnp.where(visible, jnp.exp(scores), 0.0), axis=-1))
    probability = jnp.where(visible, jnp.exp(scores - log_total[:, :, None]), 0.0)
    prob_b = probability.astype(BF16)
    context = jnp.einsum("hqk,khd->qhd", prob_b, values, preferred_element_type=F32)
    context = context.astype(BF16).reshape(seq_len, half_width)

    step = seq_len // CHUNKS
    rows_of = lambda array, chunk: array[chunk * step : (chunk + 1) * step]
    span = range(CHUNKS)

    def pair_sum(partial):
        return partial + swap_pair(partial.astype(BF16)).astype(F32)

    partials = [dot(rows_of(context, c), out_rows, ((1,), (1,))) for c in span]
    residual = [
        rows_of(rows_in, c).astype(F32) + pair_sum(partials[c]) + out_bias for c in span
    ]
    normed_one, inv_one, middle, middle_b = [], [], [], []
    pre_active, active, partials = [], [], []
    for c in span:
        normed, inv = norm_forward(residual[c])
        normed_one.append(normed)
        inv_one.append(inv)
        middle.append(normed * gain_one + shift_one)
        middle_b.append(middle[c].astype(BF16))
        pre_active.append(dot(middle_b[c], up_rows) + local_up_bias)
        tail = 0.5 * (1.0 + lax.erf(pre_active[c] * ROOT_HALF))
        active.append((pre_active[c] * tail).astype(BF16))
        partials.append(dot(active[c], down_rows, ((1,), (1,))))
    results, grad_summed, summed_b, pre_b, grad_pre, upstreams, normed_two = [], [], [], [], [], [], []
    backs = []
    for c in span:
        summed = middle[c] + pair_sum(partials[c]) + low_bias
        normed, inv = norm_forward(summed)
        normed_two.append(normed)
        results.append((normed * gain_two + shift_two).astype(BF16))
        upstreams.append(rows_of(rows_cotan, c).astype(F32))
        grad_summed.append(norm_backward(upstreams[c], normed, inv, gain_two))
        summed_b.append(grad_summed[c].astype(BF16))
        grad_active = dot(summed_b[c], down_rows)
        pre = pre_active[c]
        slope = 0.5 * (1.0 + lax.erf(pre * ROOT_HALF)) + pre * jnp.exp(-0.5 * pre * pre) * INV_ROOT_TAU
        grad_pre.append(grad_active * slope)
        pre_b.append(grad_pre[c].astype(BF16))
        backs.append(dot(pre_b[c], up_rows, ((1,), (1,))))
    join = lambda parts: jnp.concatenate(parts, axis=0)
    weight_grad = lambda left, right: dot(left, right, ((0,), (0,))) * grad_scale
    down_share = scatter_rows(weight_grad(join(summed_b), join(active)), phases)
    up_share = scatter_rows(weight_grad(join(middle_b), join(pre_b)), phases)

    grad_middle, grad_residual, residual_b, grad_context = [], [], [], []
    for c in span:
        grad_middle.append(grad_summed[c] + pair_sum(backs[c]))
        grad_residual.append(norm_backward(grad_middle[c], normed_one[c], inv_one[c], gain_one))
        residual_b.append(grad_residual[c].astype(BF16))
        grad_context.append(dot(residual_b[c], out_rows).astype(BF16))
    out_share = scatter_rows(weight_grad(join(residual_b), context), phases)

    grad_context = join(grad_context).reshape(seq_len, heads, HEAD_DIM)
    grad_prob = jnp.einsum("qhd,khd->hqk", grad_context, values, preferred_element_type=F32)
    inner = jnp.sum(probability * grad_prob, axis=-1, keepdims=True)
    grad_score = (probability * (grad_prob - inner)).astype(BF16)
    grad_query = jnp.einsum("hqk,khd->qhd", grad_score, keys, preferred_element_type=F32) * factor
    grad_key = jnp.einsum("hqk,qhd->khd", grad_score, queries, preferred_element_type=F32) * factor
    grad_value = jnp.einsum("hqk,qhd->khd", prob_b, grad_context, preferred_element_type=F32)
    proj_b = jnp.stack([grad_query, grad_key, grad_value], axis=1).astype(BF16)
    proj_b = proj_b.reshape(seq_len, 3 * half_width)
    in_share = scatter_rows(weight_grad(rows_in, proj_b), phases)

    def mine_of(parts):
        whole = join(parts)
        return jnp.where(member == 0, whole[:local_rows], whole[local_rows:])

    def other_of(parts):
        whole = join(parts)
        return jnp.where(member == 0, whole[local_rows:], whole[:local_rows])

    back = dot(proj_b, in_rows, ((1,), (1,)))
    from_pair = swap_pair(other_of([back]).astype(BF16)).astype(F32)
    my_residual = mine_of(grad_residual)
    input_grad = exact(my_residual + mine_of([back]) + from_pair, ((1,), (1,)))

    result = dot(mine_of(results), pick, ((1,), (1,))).astype(BF16)

    my_middle, my_upstream = mine_of(grad_middle), mine_of(upstreams)
    wide = exact(
        jnp.stack(
            [
                jnp.sum(my_residual, axis=0),
                jnp.sum(my_middle * mine_of(normed_one), axis=0),
                jnp.sum(my_middle, axis=0),
                jnp.sum(mine_of(grad_summed), axis=0),
                jnp.sum(my_upstream * mine_of(normed_two), axis=0),
                jnp.sum(my_upstream, axis=0),
            ]
        )
        * grad_scale,
        ((1,), (1,)),
    )
    query_sum = jnp.sum(grad_query, axis=0).reshape(half_width) * grad_scale
    value_sum = jnp.sum(grad_value, axis=0).reshape(half_width) * grad_scale
    hidden_sum = tree_sum([jnp.sum(part, axis=0) for part in grad_pre]) * grad_scale
    smalls = all_sum(
        jnp.concatenate(
            [
                wide.reshape(-1),
                placed(query_sum, width, offset),
                placed(value_sum, width, offset),
                placed(hidden_sum, 2 * hidden_half, hidden_offset),
            ]
        ),
        phases,
    )
    at = lambda index: smalls[index * width : (index + 1) * width]
    return (
        result,
        input_grad,
        in_share.reshape(block, 3, half_width),
        at(6),
        at(7),
        out_share.T,
        at(0),
        at(1),
        at(2),
        up_share,
        smalls[8 * width :],
        down_share.T,
        at(3),
        at(4),
        at(5),
    )


def solution(mesh):
    rows, whole = P(("dp", "tensor"), None), P()
    by_row, by_column = P("dp", "tensor"), P("tensor", "dp")
    by_part = P("dp", None, "tensor")
    return jax.shard_map(
        local,
        mesh=mesh,
        in_specs=(
            rows, rows, whole, P("dp"), by_part, whole, whole, by_column, whole,
            whole, whole, by_row, whole, by_column, whole, whole, whole,
        ),
        out_specs=(
            rows, rows, by_part, whole, whole, by_column, whole, whole, whole,
            by_row, whole, by_column, whole, whole, whole,
        ),
        check_vma=False,
    )
```

```python
import functools
import math

import jax
import jax.numpy as jnp
import numpy as np
from jax import lax
from jax.experimental import pallas as pl
from jax.experimental.pallas import tpu as pltpu
from jax.sharding import PartitionSpec as P


HEAD_DIM = 64
CHUNKS = 2
EPSILON = 1e-05
ROOT_HALF = 0.7071067811865476
INV_ROOT_TAU = 0.3989422804014327
LOG2_E = 1.4426950408889634


BF16 = jnp.bfloat16
F32 = jnp.float32


def strides_of(count):
    return [1 << bit for bit in range(count.bit_length() - 1)]


def block_order(strides):
    order = [0]
    for stride in reversed(strides):
        order = order + [old ^ stride for old in order]
    return order


def swap(value, distance):
    count = lax.axis_size("dp")
    return lax.ppermute(value, "dp", [(i, i ^ distance) for i in range(count)])


def swap_pair(value):
    return lax.ppermute(value, "tensor", [(0, 1), (1, 0)])


def tree_sum(parts):
    while len(parts) > 1:
        parts = [parts[i] + parts[i + 1] for i in range(0, len(parts), 2)]
    return parts[0]


def dot(left, right, dims=((1,), (0,))):
    return lax.dot_general(left, right, (dims, ((), ())), preferred_element_type=F32)


NT = ((1,), (1,))
TN = ((0,), (0,))


def shape(*dims, dtype=F32):
    return jax.ShapeDtypeStruct(dims, dtype)


def call(body, outs, args, scalars=0, far=(), scratch=()):
    def space(index):
        if index < scalars:
            return pltpu.SMEM
        return pl.ANY if index in far else pltpu.VMEM

    return pl.pallas_call(
        body,
        out_shape=outs,
        in_specs=[pl.BlockSpec(memory_space=space(i)) for i in range(len(args))],
        out_specs=jax.tree.map(lambda _: pl.BlockSpec(memory_space=pltpu.VMEM), outs),
        scratch_shapes=list(scratch),
    )(*args)


def fetch(parts, whole, sems):
    size = parts[0].shape[0]
    copies = [
        pltpu.make_async_copy(part, whole.at[pl.ds(index * size, size), :], sems.at[index])
        for index, part in enumerate(parts)
    ]
    for copy in copies:
        copy.start()
    return copies


def settle(copies):
    for copy in copies:
        copy.wait()


def room(parts):
    rows, columns = parts[0].shape
    return [
        pltpu.VMEM((rows * len(parts), columns), parts[0].dtype),
        pltpu.SemaphoreType.DMA((len(parts),)),
    ]


def stack_rows(parts):
    first = parts[0]
    pieces = first.shape[0] if first.ndim == 3 else 1
    rows, lanes = first.shape[-2:]
    aligned = rows % 16 == 0

    def body(*refs):
        if aligned:
            *ins, out, sems = refs
        else:
            *ins, out = refs
        copies = []
        for index, ref in enumerate(ins):
            for piece in range(pieces):
                source = ref.at[piece] if first.ndim == 3 else ref
                target = out.at[index * rows : (index + 1) * rows, piece * lanes : (piece + 1) * lanes]
                if aligned:
                    copy = pltpu.make_async_copy(source, target, sems.at[len(copies)])
                    copy.start()
                    copies.append(copy)
                else:
                    target[...] = source[...]
        settle(copies)

    out = shape(rows * len(parts), lanes * pieces, dtype=first.dtype)
    if not aligned:
        return call(body, out, parts)
    scratch = [pltpu.SemaphoreType.DMA((len(parts) * pieces,))]
    return call(body, out, parts, far=range(len(parts)), scratch=scratch)


def gather_rows(shard, strides):
    low, high = strides[-2:]
    held = stack_rows([shard] + [swap(shard, step) for step in (high, low, low ^ high)])
    for stride in reversed(strides[2:-2]):
        held = stack_rows([held, swap(held, stride)])
    parts = [held, swap(held, strides[1])]
    return parts + [swap(part, strides[0]) for part in parts]


def fold(keep, received, cut, shares=None):
    rows, columns = keep.shape
    size = rows // cut

    def body(*refs):
        keep_ref, *rest = refs
        ins, outs = rest[: len(received)], rest[len(received) :]
        if shares:
            total = tree_sum([keep_ref[...].astype(F32)] + [ref[...].astype(F32) for ref in ins])
            at = 0
            for out in outs:
                lanes = out.shape[-1]
                for part in range(out.shape[0]):
                    out[part] = total[:, at : at + lanes]
                    at += lanes
            return
        for index, out in enumerate(outs):
            where = slice(index * size, (index + 1) * size)
            terms = [keep_ref[where, :].astype(F32)] + [ref[where, :].astype(F32) for ref in ins]
            out[...] = tree_sum(terms).astype(BF16)

    if shares:
        outs = [shape(parts, rows, columns_of) for parts, columns_of in shares]
    else:
        outs = [shape(size, columns, dtype=BF16)] * cut
    return call(body, outs, [keep, *received])


def scatter_rows(keep, send, strides, shares, direct):
    received = [swap(send, strides[0])]
    for stride in strides[1 : -2 if direct else None]:
        keep, send = fold(keep, received, 2)
        received = [swap(send, stride)]
    if direct:
        low, high = strides[-2:]
        keep, *sends = fold(keep, received, 4)
        received = [swap(piece, step) for piece, step in zip(sends, (high, low, low ^ high))]
    return fold(keep, received, 1, shares)


def all_sum(vector, strides):
    low, high = strides[-2:]
    vector = tree_sum([vector] + [swap(vector, step) for step in (low, high, low ^ high)])
    for stride in strides[:-2]:
        vector = vector + swap(vector, stride)
    return vector + swap_pair(vector)


def normalize(values):
    centered = values - jnp.mean(values, axis=-1, keepdims=True)
    inv_std = lax.rsqrt(jnp.mean(centered * centered, axis=-1, keepdims=True) + EPSILON)
    return centered * inv_std, inv_std


def norm_backward(upstream, normed, inv_std, gain):
    scaled = upstream * gain
    return inv_std * (
        scaled
        - jnp.mean(scaled, axis=-1, keepdims=True)
        - normed * jnp.mean(scaled * normed, axis=-1, keepdims=True)
    )


def row_sum(values):
    return jnp.sum(values, axis=0, keepdims=True)


def attend_body(length, member, mine, other, bias, *refs):
    weights = refs[:4]
    rows, proj, probs, context, *partials = refs[4:-2]
    whole, sems = refs[-2:]
    copies = fetch(weights, whole, sems)
    local_rows = mine.shape[0]
    seq_len, wide = proj.shape
    half_width = wide // 3
    pair = 2 * HEAD_DIM
    factor = LOG2_E / math.sqrt(HEAD_DIM)
    visible = lax.broadcasted_iota(jnp.int32, (seq_len, 1), 0) < length[0]
    low_lane = lax.broadcasted_iota(jnp.int32, (1, pair), 1) < HEAD_DIM
    first = pl.multiple_of(member[0] * local_rows, local_rows)
    second = pl.multiple_of((1 - member[0]) * local_rows, local_rows)
    rows[pl.ds(first, local_rows), :] = mine[...]
    rows[pl.ds(second, local_rows), :] = other[...]
    settle(copies)
    proj[...] = (dot(rows[...], whole[:, :wide]) + bias[...]).astype(BF16)
    for tile in range(half_width // pair):
        at = slice(tile * pair, (tile + 1) * pair)
        query = proj[:, at]
        key = proj[:, half_width + tile * pair : half_width + (tile + 1) * pair]
        value = proj[:, 2 * half_width + tile * pair : 2 * half_width + (tile + 1) * pair]
        turned = value.astype(F32).T.astype(BF16)
        pieces = []
        for side in range(2):
            lanes = low_lane if side == 0 else ~low_lane
            scores = dot(jnp.where(lanes, key, 0), query, NT) * factor
            grown = jnp.where(visible, jnp.exp2(scores), 0.0)
            log_total = jnp.log2(row_sum(grown))
            prob = jnp.where(visible, jnp.exp2(scores - log_total), 0.0).astype(BF16)
            probs[2 * tile + side] = prob
            pieces.append(dot(turned[side * HEAD_DIM : (side + 1) * HEAD_DIM], prob))
        context[:, at] = jnp.concatenate(pieces, axis=0).T.astype(BF16)
    step = seq_len // CHUNKS
    for chunk in range(CHUNKS):
        part = dot(context[chunk * step : (chunk + 1) * step, :], whole[:, wide:], NT)
        partials[2 * chunk][...] = part
        partials[2 * chunk + 1][...] = part.astype(BF16)


def head_grads(tiles, proj, probs, context, grad_in, grads, head_sums):
    wide = proj.shape[1]
    half_width = wide // 3
    pair = 2 * HEAD_DIM
    factor = 1.0 / math.sqrt(HEAD_DIM)
    low_lane = lax.broadcasted_iota(jnp.int32, (1, pair), 1) < HEAD_DIM
    for tile in tiles:
        at = slice(tile * pair, (tile + 1) * pair)
        at_key = slice(half_width + tile * pair, half_width + (tile + 1) * pair)
        at_value = slice(2 * half_width + tile * pair, 2 * half_width + (tile + 1) * pair)
        query, key, value = proj[:, at], proj[:, at_key], proj[:, at_value]
        grad = grad_in[:, at]
        product = (grad.astype(F32) * context[:, at].astype(F32)).T
        key_turned = key.astype(F32).T.astype(BF16)
        query_parts, key_grad, value_grad = [], 0.0, 0.0
        for side in range(2):
            lanes = low_lane if side == 0 else ~low_lane
            here = slice(side * HEAD_DIM, (side + 1) * HEAD_DIM)
            prob = probs[2 * tile + side]
            inner = row_sum(product[here])
            grad_prob = dot(jnp.where(lanes, value, 0), grad, NT)
            grad_score = (prob.astype(F32) * (grad_prob - inner)).astype(BF16)
            query_parts.append(dot(key_turned[here], grad_score))
            key_grad = key_grad + dot(grad_score, jnp.where(lanes, query, 0))
            value_grad = value_grad + dot(prob, jnp.where(lanes, grad, 0))
        query_grad = jnp.concatenate(query_parts, axis=0).T * factor
        grads[:, at] = query_grad.astype(BF16)
        grads[:, at_key] = (key_grad * factor).astype(BF16)
        grads[:, at_value] = value_grad.astype(BF16)
        head_sums[0:1, at] = row_sum(query_grad)
        head_sums[1:2, at] = row_sum(value_grad)


def heads_body(tiles, proj, probs, context, vectors, *refs):
    chunks = [refs[5 * c : 5 * c + 5] for c in range(CHUNKS)]
    weights = refs[5 * CHUNKS : 5 * CHUNKS + 4]
    residual_out, sums, grads, head_sums, residual_b, grad_in, whole, sems = refs[5 * CHUNKS + 4 :]
    copies = fetch(weights, whole, sems)
    seq_len, wide = proj.shape
    step = seq_len // CHUNKS
    for c, (grad, mine, other, normed, inv_std) in enumerate(chunks):
        cut = slice(c * step, (c + 1) * step)
        grad_middle = grad[...] + (mine[...] + other[...].astype(F32))
        sums[c, 0:1, :] = row_sum(grad_middle * normed[...])
        sums[c, 1:2, :] = row_sum(grad_middle)
        residual = norm_backward(grad_middle, normed[...], inv_std[...], vectors[1:2, :])
        sums[c, 2:3, :] = row_sum(residual)
        residual_out[cut, :] = residual
        residual_b[cut, :] = residual.astype(BF16)
    settle(copies)
    grad_in[...] = dot(residual_b[...], whole[:, wide:]).astype(BF16)
    head_grads(tiles, proj, probs, context, grad_in, grads, head_sums)


def heads_more_body(done, tiles, scale, proj, probs, context, rows, residual_b, grad_in, early, early_sums,
                    grads, head_sums, keep, send):
    wide = proj.shape[1]
    half_width = wide // 3
    for part in range(3):
        at = slice(part * half_width, part * half_width + done)
        grads[:, at] = early[:, at]
    head_sums[:, :done] = early_sums[:, :done]
    head_grads(tiles, proj, probs, context, grad_in, grads, head_sums)
    half = keep.shape[0]
    for index, out in ((1, send), (0, keep)):
        cut = slice(index * half, (index + 1) * half)
        out[:, :wide] = (dot(rows[:, cut], grads[...], TN) * scale).astype(BF16)
        out[:, wide:] = (dot(residual_b[:, cut], context[...], TN) * scale).astype(BF16)


def middle_of(normed, vectors):
    return normed * vectors[1:2, :] + vectors[2:3, :]


def feed_body(chunk, rows, mine, other, vectors, bias, *refs):
    ups, downs = refs[:4], refs[4:8]
    normed_out, inv_out, middle_out, active_out, slope_out, keep, send = refs[8:-4]
    up, sems, down, sems_down = refs[-4:]
    copies, later = fetch(ups, up, sems), fetch(downs, down, sems_down)
    step = mine.shape[0]
    residual = rows[chunk * step : (chunk + 1) * step, :].astype(F32) + (mine[...] + other[...].astype(F32)) + vectors[0:1, :]
    normed, inv_std = normalize(residual)
    normed_out[...] = normed
    inv_out[...] = inv_std
    middle_b = middle_of(normed, vectors).astype(BF16)
    middle_out[...] = middle_b
    settle(copies)
    pre = dot(middle_b, up[...]) + bias[...]
    tail = 0.5 * (1.0 + lax.erf(pre * ROOT_HALF))
    active = (pre * tail).astype(BF16)
    active_out[...] = active
    slope_out[...] = (tail + pre * jnp.exp2(pre * pre * (-0.5 * LOG2_E)) * INV_ROOT_TAU).astype(BF16)
    settle(later)
    part = dot(active, down[...], NT)
    keep[...] = part
    send[...] = part.astype(BF16)


def feed_back_body(chunk, member, normed_in, mine, other, my_cotan, other_cotan, vectors, slope, *refs):
    ups, downs = refs[:4], refs[4:8]
    result, grad_out, summed_out, pre_out, keep, send, sums, hidden = refs[8:-4]
    up, sems, down, sems_down = refs[-4:]
    copies, later = fetch(downs, down, sems_down), fetch(ups, up, sems)
    summed = middle_of(normed_in[...], vectors) + (mine[...] + other[...].astype(F32)) + vectors[3:4, :]
    normed, inv_std = normalize(summed)
    result[...] = (normed * vectors[4:5, :] + vectors[5:6, :]).astype(BF16)
    upstream = jnp.where(member[0] == chunk, my_cotan[...], other_cotan[...]).astype(F32)
    grad = norm_backward(upstream, normed, inv_std, vectors[4:5, :])
    grad_out[...] = grad
    sums[0:1, :] = row_sum(grad)
    sums[1:2, :] = row_sum(upstream * normed)
    sums[2:3, :] = row_sum(upstream)
    grad_b = grad.astype(BF16)
    summed_out[...] = grad_b
    settle(copies)
    pre = dot(grad_b, down[...]) * slope[...].astype(F32)
    hidden[...] = row_sum(pre)
    pre_b = pre.astype(BF16)
    pre_out[...] = pre_b
    settle(later)
    part = dot(pre_b, up[...], NT)
    keep[...] = part
    send[...] = part.astype(BF16)


def weight_body(scale, count, *refs):
    lefts, rights = refs[:count], refs[count:-2]
    keep, send = refs[-2:]
    half = keep.shape[0]
    right = jnp.concatenate([ref[...] for ref in rights], axis=0)
    for index, out in ((1, send), (0, keep)):
        left = jnp.concatenate([ref[:, index * half : (index + 1) * half] for ref in lefts], axis=0)
        out[...] = (dot(left, right, TN) * scale).astype(BF16)


def weight_grad(lefts, rights, scale):
    width, columns = lefts[0].shape[1], rights[0].shape[1]
    return call(
        functools.partial(weight_body, scale, len(lefts)),
        [shape(width // 2, columns, dtype=BF16)] * 2,
        [*lefts, *rights],
    )


def back_body(member, grads, *refs):
    weights = refs[:4]
    mine, other, whole, sems = refs[4:]
    copies = fetch(weights, whole, sems)
    rows, wide = mine.shape[0], grads.shape[1]
    settle(copies)
    for out, start in ((other, 1 - member[0]), (mine, member[0])):
        piece = grads[pl.ds(pl.multiple_of(start * rows, rows), rows), :]
        out[...] = dot(piece, whole[:, :wide], NT).astype(out.dtype)


def unpick(values, pick):
    whole = 0.0
    for _ in range(3):
        part = values.astype(BF16)
        values = values - part.astype(F32)
        whole = whole + dot(part, pick[...], NT)
    return whole


def finish_body(member, residual, mine, other, pick, *refs):
    results, (out, result) = refs[:CHUNKS], refs[CHUNKS:]
    rows = out.shape[0]
    own = residual[pl.ds(pl.multiple_of(member[0] * rows, rows), rows), :]
    out[...] = unpick(own + mine[...] + other[...].astype(F32), pick)
    mine_result = jnp.where(member[0] == 0, results[0][...], results[1][...])
    result[...] = dot(mine_result, pick[...], NT).astype(BF16)


def totals_body(scale, member, firsts, head_sums, pick, *refs):
    lows, hiddens, out = refs[:CHUNKS], refs[CHUNKS : 2 * CHUNKS], refs[-1]
    is_first = member[0] == 0
    width = firsts.shape[2]
    half_width, hidden_half = head_sums.shape[1], hiddens[0].shape[1]
    wide = jnp.concatenate(
        [
            jnp.where(is_first, firsts[0], firsts[1]),
            jnp.where(is_first, lows[0][...], lows[1][...]),
            jnp.zeros((2, width), F32),
        ],
        axis=0,
    )
    out[0:8, :] = unpick(wide * scale, pick)
    empty = jnp.zeros((1, half_width), F32)
    for row in range(2):
        line = head_sums[row : row + 1, :] * scale
        out[6 + row : 7 + row, :] = jnp.where(
            is_first, jnp.concatenate([line, empty], axis=1), jnp.concatenate([empty, line], axis=1)
        )
    hidden = (hiddens[0][...] + hiddens[1][...]) * scale
    per_side = hidden_half // width
    for row in range(2 * per_side):
        at = row % per_side
        line = hidden[:, at * width : (at + 1) * width]
        out[8 + row : 9 + row, :] = jnp.where(is_first == (row < per_side), line, 0.0)


def local(
    layer_in,
    cotangent,
    lengths,
    slot_sequence,
    input_proj,
    query_bias,
    value_bias,
    output_proj,
    output_bias,
    first_gain,
    first_shift,
    up_proj,
    up_bias,
    down_proj,
    down_bias,
    second_gain,
    second_shift,
):
    me = lax.axis_index("dp")
    member = lax.axis_index("tensor")
    count = lax.axis_size("dp")
    strides = strides_of(count)
    local_rows, width = layer_in.shape
    seq_len = local_rows * 2
    half_width = input_proj.shape[2]
    heads = half_width // HEAD_DIM
    hidden_half = up_proj.shape[1]
    block = input_proj.shape[0]
    grad_scale = 1.0 / math.sqrt(seq_len * count)
    offset = member * half_width
    hidden_offset = member * hidden_half
    length = jnp.sum(jnp.where(jnp.arange(lengths.shape[0]) == slot_sequence[0], lengths, 0))

    order = np.repeat(np.asarray(block_order(strides), np.int32), block)
    source = (me ^ order) * block + np.arange(width, dtype=np.int32) % block
    pick = (jnp.arange(width)[:, None] == source[None, :]).astype(BF16)

    def exact(values, dims):
        return lax.dot_general(
            values,
            pick.astype(F32),
            (dims, ((), ())),
            precision=lax.Precision.HIGHEST,
            preferred_element_type=F32,
        )

    io_shard = jnp.concatenate([input_proj.transpose(1, 0, 2), output_proj.T[None]], axis=0)
    ios = gather_rows(io_shard, strides)
    ups = gather_rows(up_proj, strides)
    downs = gather_rows(down_proj.T, strides)

    vectors = exact(
        jnp.stack([output_bias, first_gain, first_shift, down_bias, second_gain, second_shift]),
        ((1,), (0,)),
    )

    mine_in = dot(layer_in, pick).astype(BF16)
    other_in = swap_pair(mine_in)
    mine_cotan = dot(cotangent, pick).astype(BF16)
    other_cotan = swap_pair(mine_cotan)
    member_at = member.reshape(1)

    proj_bias = jnp.concatenate(
        [
            lax.dynamic_slice_in_dim(query_bias, offset, half_width),
            jnp.zeros((half_width,), F32),
            lax.dynamic_slice_in_dim(value_bias, offset, half_width),
        ]
    )[None, :]
    local_up_bias = lax.dynamic_slice_in_dim(up_bias, hidden_offset, hidden_half)[None, :]

    step = seq_len // CHUNKS
    span = range(CHUNKS)
    wide, thin = shape(step, width), shape(step, width, dtype=BF16)
    hidden_b = shape(step, hidden_half, dtype=BF16)
    flat_b = shape(seq_len, 3 * half_width, dtype=BF16)

    rows_in, proj, probs, context, *first = call(
        attend_body,
        [shape(seq_len, width, dtype=BF16), flat_b, shape(heads, seq_len, seq_len, dtype=BF16),
         shape(seq_len, half_width, dtype=BF16)]
        + [wide, thin] * CHUNKS,
        [length.reshape(1), member_at, mine_in, other_in, proj_bias, *ios],
        scalars=2,
        far=range(5, 9),
        scratch=room(ios),
    )
    first_other = [swap_pair(first[2 * c + 1]) for c in span]
    fed = [
        call(
            functools.partial(feed_body, c),
            [wide, shape(step, 1), thin, hidden_b, hidden_b, wide, thin],
            [rows_in, first[2 * c], first_other[c], vectors, local_up_bias, *ups, *downs],
            far=range(5, 13),
            scratch=room(ups) + room(downs),
        )
        for c in span
    ]
    second_other = [swap_pair(fed[c][6]) for c in span]
    backs = [
        call(
            functools.partial(feed_back_body, c),
            [thin, wide, thin, hidden_b, wide, thin, shape(3, width), shape(1, hidden_half)],
            [member_at, fed[c][0], fed[c][5], second_other[c], mine_cotan, other_cotan, vectors, fed[c][4],
             *ups, *downs],
            scalars=1,
            far=range(8, 16),
            scratch=room(ups) + room(downs),
        )
        for c in span
    ]
    third_other = [swap_pair(backs[c][5]) for c in span]
    (down_share,) = scatter_rows(
        *weight_grad([backs[c][2] for c in span], [fed[c][3] for c in span], grad_scale),
        strides, [(1, hidden_half)], False,
    )
    (up_share,) = scatter_rows(
        *weight_grad([fed[c][2] for c in span], [backs[c][3] for c in span], grad_scale),
        strides, [(1, hidden_half)], False,
    )
    tiles = half_width // (2 * HEAD_DIM)
    early = max(tiles - 1, 1)
    residual_grad, first_sums, early_grads, early_sums, residual_b, grad_context = call(
        functools.partial(heads_body, range(early)),
        [shape(seq_len, width), shape(CHUNKS, 3, width), flat_b, shape(2, half_width),
         shape(seq_len, width, dtype=BF16), shape(seq_len, half_width, dtype=BF16)],
        [proj, probs, context, vectors]
        + [item for c in span for item in (backs[c][1], backs[c][4], third_other[c], fed[c][0], fed[c][1])]
        + ios,
        far=range(4 + 5 * CHUNKS, 8 + 5 * CHUNKS),
        scratch=room(ios),
    )
    proj_b, head_sums, *io_grads = call(
        functools.partial(heads_more_body, early * 2 * HEAD_DIM, range(early, tiles), grad_scale),
        [flat_b, shape(2, half_width)] + [shape(width // 2, 4 * half_width, dtype=BF16)] * 2,
        [proj, probs, context, rows_in, residual_b, grad_context, early_grads, early_sums],
    )
    in_share, out_share = scatter_rows(*io_grads, strides, [(3, half_width), (1, half_width)], True)
    kept, sent = call(
        back_body,
        [shape(local_rows, width), shape(local_rows, width, dtype=BF16)],
        [member_at, proj_b, *ios],
        scalars=1,
        far=range(2, 6),
        scratch=room(ios),
    )
    from_pair = swap_pair(sent)

    input_grad, result = call(
        finish_body,
        [shape(local_rows, width), shape(local_rows, width, dtype=BF16)],
        [member_at, residual_grad, kept, from_pair, pick, *[b[0] for b in backs]],
        scalars=1,
    )
    totals = call(
        functools.partial(totals_body, grad_scale),
        shape(8 + 2 * (hidden_half // width), width),
        [member_at, first_sums, head_sums, pick, *[b[6] for b in backs], *[b[7] for b in backs]],
        scalars=1,
    )
    smalls = all_sum(totals, strides)
    at = lambda index: smalls[index]
    return (
        result,
        input_grad,
        in_share.transpose(1, 0, 2),
        at(6),
        at(7),
        out_share[0].T,
        at(2),
        at(0),
        at(1),
        up_share[0],
        smalls[8:].reshape(-1),
        down_share[0].T,
        at(3),
        at(4),
        at(5),
    )


def solution(mesh):
    rows, whole = P(("dp", "tensor"), None), P()
    by_row, by_column = P("dp", "tensor"), P("tensor", "dp")
    by_part = P("dp", None, "tensor")
    return jax.shard_map(
        local,
        mesh=mesh,
        in_specs=(
            rows, rows, whole, P("dp"), by_part, whole, whole, by_column, whole,
            whole, whole, by_row, whole, by_column, whole, whole, whole,
        ),
        out_specs=(
            rows, rows, by_part, whole, whole, by_column, whole, whole, whole,
            by_row, whole, by_column, whole, whole, whole,
        ),
        check_vma=False,
    )
```
